32 devices in a mesh: region: 4 (over y, core), local: 8 (over z, x).
Axes of the slice: x: 2, y: 2, z: 4, core: 2. Of those that a mesh axis runs over, the one named last changes fastest.
Arguments:
- distributions: float32 [96, 19, 4096], P(('region', 'local')), may hold values from 0.5 to 1.5
- fluid: int32 [96, 4096], P(('region', 'local')), may hold values 0 or 1
- boundary: float32 [32, 2, 5, 256], P(('region', 'local')), may hold values from 0.5 to 1.5
- face_link: int32 [32, 6], P(('region', 'local')), may hold values from 0 to 11, as said below
- move_slot: int32 [32, 1], P(('region', 'local')), may hold values from 0 to 2, as said below
Outputs:
- distributions_out: float32 [96, 19, 4096], P(('region', 'local'))
The draws below stay inside these ranges and needn't reach their ends.
Inputs may be any that keep to these rules, and one draw needn't show every extreme that they name: `face_link`: on every device, each port toward an existing neighbour device is used by exactly one face, and no port toward a missing neighbour is used; exactly two faces read the boundary planes (values 2 * 3 + 4 * 1 and that plus one); every other face names another face of the same device. `move_slot`: the 1 slots of a device are distinct.
All inputs are finite; a program needn't handle non-finite values. No bound on the sum of `fluid` on one device may be relied on, other than what follows from the above.
Results may differ from the reference program's by a relative error of at most 0.0001.
Values sent between devices are 32-bit elements; how exact they have to be, the bound alone decides.
A program may use at most 64 MiB of HBM per device.

```python
import jax
import jax.numpy as jnp
from jax import lax

EDGE = 16
BLOCKS_DEV = 3
PORTS_DIR = 1
MOVED = 1
ITERS = 2
PLANE = 256
SITES = 4096
SLOTS = 96
N_REGION = 4
N_LOCAL = 8
DEVICES = 32


def draw_face_link(key, part):
    face_count = 2 * BLOCKS_DEV
    dev_count = N_REGION * N_LOCAL
    scores = jax.random.randint(jax.random.fold_in(key, 11), (dev_count, face_count), 0, 1 << 20) * face_count + jnp.arange(face_count, dtype=jnp.int32)[None, :]
    order = jnp.argsort(scores, axis=1).astype(jnp.int32)
    position = jnp.arange(face_count, dtype=jnp.int32)
    device_ids = jnp.arange(dev_count, dtype=jnp.int32)
    region_idx = device_ids // N_LOCAL
    local_idx = device_ids % N_LOCAL
    exists = jnp.stack([local_idx > 0, local_idx < N_LOCAL - 1, region_idx > 0, region_idx < N_REGION - 1], 1)
    direction = jnp.minimum(position // PORTS_DIR, 3)
    is_port = (position[None, :] < 4 * PORTS_DIR) & exists[:, direction]
    paired = jnp.take_along_axis(order, jnp.broadcast_to(jnp.bitwise_xor(position, 1)[None, :], (dev_count, face_count)), axis=1)
    opened = face_count + 4 * PORTS_DIR + position - (face_count - 2)
    value = jnp.where(is_port, face_count + position[None, :], jnp.where(position[None, :] < face_count - 2, paired, opened[None, :]))
    link = jnp.zeros((dev_count, face_count), jnp.int32).at[device_ids[:, None], order].set(value.astype(jnp.int32))
    return link


def draw_move_slot(key, part):
    dev_count = N_REGION * N_LOCAL
    scores = jax.random.randint(jax.random.fold_in(key, 23), (dev_count, BLOCKS_DEV), 0, 1 << 20) * BLOCKS_DEV + jnp.arange(BLOCKS_DEV, dtype=jnp.int32)[None, :]
    order = jnp.argsort(scores, axis=1).astype(jnp.int32)
    return order[:, :MOVED]


def plant(values, stream_key, low, high):
    longest = values.shape.index(max(values.shape))
    spots = []
    for shift in (0, 1):
        where = [jax.random.randint(jax.random.fold_in(stream_key, axis), (), 0, length) for axis, length in enumerate(values.shape)]
        where[longest] = (where[longest] + shift) % values.shape[longest]
        spots.append(tuple(where))
    return values.at[spots[0]].set(low).at[spots[1]].set(high)


def steps_of(stream_key, dims, cuts, smallest, high):
    loudness = 1.0
    for dim, shards_of in cuts:
        draws = jax.random.uniform(jax.random.fold_in(jax.random.fold_in(stream_key, 6), dim), (shards_of,), jnp.float32, smallest / len(cuts), high / len(cuts))
        loudness = loudness * jnp.repeat(jnp.exp(draws), dims[dim] // shards_of).reshape((-1,) + (1,) * (len(dims) - 1 - dim))
    return loudness


def setup_inputs(seed: int = 0) -> dict:
    streams_of = jax.random.split(jax.random.key(seed), 6)
    return {
        "distributions": jnp.clip(0.5 + 1.0 * jax.random.uniform(streams_of[0], (SLOTS, 19, SITES), jnp.float32) ** steps_of(streams_of[0], (SLOTS, 19, SITES), ((0, 32),), -0.2, 0.2), 0.5, 1.5),
        "fluid": plant((jax.random.randint(streams_of[1], (SLOTS, SITES), 0, 8) < 7).astype(jnp.int32), jax.random.fold_in(streams_of[1], 1), 0, 1),
        "boundary": jnp.clip(0.5 + 1.0 * jax.random.uniform(streams_of[2], (DEVICES, 2, 5, PLANE), jnp.float32) ** steps_of(streams_of[2], (DEVICES, 2, 5, PLANE), ((0, 32),), -0.2, 0.2), 0.5, 1.5),
        "face_link": draw_face_link(jax.random.fold_in(streams_of[5], 71), 0),
        "move_slot": draw_move_slot(jax.random.fold_in(streams_of[5], 71), 0),
    }


VELOCITIES = [(0, 0, 0), (1, 0, 0), (-1, 0, 0), (0, 1, 0), (0, -1, 0), (0, 0, 1), (0, 0, -1),
              (1, 1, 0), (-1, -1, 0), (1, -1, 0), (-1, 1, 0), (1, 0, 1), (-1, 0, -1), (1, 0, -1), (-1, 0, 1),
              (0, 1, 1), (0, -1, -1), (0, 1, -1), (0, -1, 1)]
WEIGHTS = [1.0 / 3.0] + [1.0 / 18.0] * 6 + [1.0 / 36.0] * 12
OPPOSITE = [0, 2, 1, 4, 3, 6, 5, 8, 7, 10, 9, 12, 11, 14, 13, 16, 15, 18, 17]
PLUS_POPS = [1, 7, 9, 11, 13]
MINUS_POPS = [2, 10, 8, 14, 12]
OMEGA_RATE = 1.6


def collide(values):
    populations = [values[:, index] for index in range(19)]
    density = jnp.zeros_like(populations[0])
    flow_x = jnp.zeros_like(populations[0])
    flow_y = jnp.zeros_like(populations[0])
    flow_z = jnp.zeros_like(populations[0])
    for index in range(19):
        weight = WEIGHTS[index]
        velo_x, velo_y, velo_z = VELOCITIES[index]
        density = density + weight * populations[index]
        if velo_x != 0:
            flow_x = flow_x + (velo_x * weight) * populations[index]
        if velo_y != 0:
            flow_y = flow_y + (velo_y * weight) * populations[index]
        if velo_z != 0:
            flow_z = flow_z + (velo_z * weight) * populations[index]
    speed_sq = flow_x * flow_x + flow_y * flow_y + flow_z * flow_z
    results = []
    for index in range(19):
        velo_x, velo_y, velo_z = VELOCITIES[index]
        project = velo_x * flow_x + velo_y * flow_y + velo_z * flow_z
        equil = density + 3.0 * project + 4.5 * project * project - 1.5 * speed_sq
        results.append(populations[index] - OMEGA_RATE * (populations[index] - equil))
    return jnp.stack(results, 1)


def stream(collided, incoming, fluid_mask, edge_len):
    plane_len = edge_len * edge_len
    flat = jnp.arange(plane_len, dtype=jnp.int32)
    row_pos = flat // edge_len
    col_pos = flat % edge_len
    results = []
    for index in range(19):
        velo_x, velo_y, velo_z = VELOCITIES[index]
        values = collided[:, index]
        if velo_x == 1:
            place = PLUS_POPS.index(index)
            values = jnp.concatenate([incoming[:, 0, place][:, None], values[:, :-1]], 1)
            source_ok = jnp.concatenate([fluid_mask[:, :1], fluid_mask[:, :-1]], 1)
        elif velo_x == -1:
            place = MINUS_POPS.index(index)
            values = jnp.concatenate([values[:, 1:], incoming[:, 1, place][:, None]], 1)
            source_ok = jnp.concatenate([fluid_mask[:, 1:], fluid_mask[:, -1:]], 1)
        else:
            source_ok = fluid_mask
        offset = velo_y * edge_len + velo_z
        if offset != 0:
            values = jnp.roll(values, offset, axis=-1)
            source_ok = jnp.roll(source_ok, offset, axis=-1)
        inside = (row_pos - velo_y >= 0) & (row_pos - velo_y < edge_len) & (col_pos - velo_z >= 0) & (col_pos - velo_z < edge_len)
        pulled = jnp.where(source_ok & inside, values, collided[:, OPPOSITE[index]])
        results.append(jnp.where(fluid_mask, pulled, jnp.zeros_like(pulled)))
    return jnp.stack(results, 1)


def reference(distributions, fluid, boundary, face_link, move_slot):
    edge_len = EDGE
    plane_len = edge_len * edge_len
    regions = N_REGION
    locals_count = N_LOCAL
    dev_count = regions * locals_count
    blocks = BLOCKS_DEV
    face_count = 2 * blocks
    port_count = 4 * PORTS_DIR
    current = distributions.reshape(dev_count, blocks, 19, edge_len * plane_len)
    device_ids = jnp.arange(dev_count, dtype=jnp.int32)
    partner = (device_ids // locals_count) * locals_count + jnp.bitwise_xor(device_ids % locals_count, locals_count // 2)
    outgoing = jnp.take_along_axis(current, move_slot[:, :, None, None], axis=1)
    arrived = outgoing[partner]
    current = current.at[device_ids[:, None], move_slot].set(arrived)
    current = current.reshape(dev_count, blocks, 19, edge_len, plane_len)
    fluid_mask = fluid.reshape(dev_count, blocks, edge_len, plane_len) > 0
    ports_hot = (face_link[:, :, None] == face_count + jnp.arange(port_count, dtype=jnp.int32)[None, None, :]).astype(jnp.float32)
    groups = dev_count // 8
    for iteration in range(ITERS):
        layers = jnp.stack([current[:, :, :, 0, :], current[:, :, :, edge_len - 1, :]], 2)
        layers = collide(layers.reshape(dev_count * face_count, 19, plane_len)).reshape(dev_count, blocks, 2, 19, plane_len)
        planes = jnp.stack([layers[:, :, 0][:, :, jnp.array(MINUS_POPS)], layers[:, :, 1][:, :, jnp.array(PLUS_POPS)]], 2)
        planes = planes.reshape(dev_count, face_count, 5, plane_len)
        sent = jnp.einsum('dfp,dfjs->dpjs', ports_hot, planes, precision=lax.Precision.HIGHEST)
        sent = sent.reshape(regions, locals_count, 4, PORTS_DIR, 5, plane_len)
        zero_local = jnp.zeros_like(sent[:, :1, 0])
        zero_region = jnp.zeros_like(sent[:1, :, 0])
        from_lower = jnp.concatenate([zero_local, sent[:, :-1, 1]], 1)
        from_upper = jnp.concatenate([sent[:, 1:, 0], zero_local], 1)
        from_below = jnp.concatenate([zero_region, sent[:-1, :, 3]], 0)
        from_above = jnp.concatenate([sent[1:, :, 2], zero_region], 0)
        received = jnp.stack([from_lower, from_upper, from_below, from_above], 2).reshape(dev_count, port_count, 5, plane_len)
        pool_rows = jnp.concatenate([planes, received, boundary], 1)
        incoming = jnp.take_along_axis(pool_rows, face_link[:, :, None, None], axis=1)
        incoming = incoming.reshape(groups, 8 * blocks, 2, 5, plane_len)

        def advance(bundle):
            return stream(collide(bundle[0]), bundle[1], bundle[2], edge_len)

        current = lax.map(advance, (current.reshape(groups, 8 * blocks, 19, edge_len, plane_len), incoming,
                                    fluid_mask.reshape(groups, 8 * blocks, edge_len, plane_len)))
        current = current.reshape(dev_count, blocks, 19, edge_len, plane_len)
    return current.reshape(dev_count * blocks, 19, edge_len * plane_len)
```

```python
import functools

import jax
import jax.numpy as jnp
from jax import lax
from jax.experimental import pallas as pl
from jax.experimental.pallas import tpu as pltpu
from jax.sharding import PartitionSpec as P

EDGE = 16
ITERS = 2
PLANE = EDGE * EDGE
HALF = EDGE // 2
QUARTER = EDGE // 4
MESH = pl.DeviceIdType.MESH

VELOCITIES = [
    (0, 0, 0),
    (1, 0, 0),
    (-1, 0, 0),
    (0, 1, 0),
    (0, -1, 0),
    (0, 0, 1),
    (0, 0, -1),
    (1, 1, 0),
    (-1, -1, 0),
    (1, -1, 0),
    (-1, 1, 0),
    (1, 0, 1),
    (-1, 0, -1),
    (1, 0, -1),
    (-1, 0, 1),
    (0, 1, 1),
    (0, -1, -1),
    (0, 1, -1),
    (0, -1, 1),
]
OPPOSITE = [0, 2, 1, 4, 3, 6, 5, 8, 7, 10, 9, 12, 11, 14, 13, 16, 15, 18, 17]
PLUS_POPS = [1, 7, 9, 11, 13]
MINUS_POPS = [2, 10, 8, 14, 12]
POPS = 19
GROUPS = [(0, 7), (7, 13), (13, 19)]


def collide(g):
    near = (g[1] + g[2]) + (g[3] + g[4]) + (g[5] + g[6])
    pair = {i: g[i] + g[i + 1] for i in range(7, POPS, 2)}
    diff = {i: g[i] - g[i + 1] for i in range(1, POPS, 2)}
    far = (pair[7] + pair[9]) + (pair[11] + pair[13]) + (pair[15] + pair[17])
    rho = (1.0 / 3.0) * g[0] + (1.0 / 18.0) * near + (1.0 / 36.0) * far
    ux = (1.0 / 18.0) * diff[1] + (1.0 / 36.0) * ((diff[7] + diff[9]) + (diff[11] + diff[13]))
    uy = (1.0 / 18.0) * diff[3] + (1.0 / 36.0) * ((diff[7] - diff[9]) + (diff[15] + diff[17]))
    uz = (1.0 / 18.0) * diff[5] + (1.0 / 36.0) * ((diff[11] - diff[13]) + (diff[15] - diff[17]))
    base = 1.6 * rho - 2.4 * (ux * ux + uy * uy + uz * uz)
    post = [base - 0.6 * g[0]]
    flows = [ux, uy, uz, ux + uy, ux - uy, ux + uz, ux - uz, uy + uz, uy - uz]
    for k, flow in enumerate(flows):
        i = 1 + 2 * k
        even = base + 7.2 * (flow * flow)
        odd = 4.8 * flow
        post.append((even + odd) - 0.6 * g[i])
        post.append((even - odd) - 0.6 * g[i + 1])
    return post


def kernel(
    n_region,
    n_local,
    link_ref,
    move_ref,
    dist_ref,
    edge_ref,
    inner_ref,
    fluid_ref,
    bound_ref,
    out_ref,
    post_ref,
    g_ref,
    slab_ref,
    slab_post_ref,
    code_ref,
    arr_edge,
    arr_inner,
    pool0,
    pool1,
    ports,
    edge_sems,
    inner_send,
    inner_recv,
    port_send,
    port_recv,
):
    pools = [pool0, pool1]
    region, local = lax.axis_index("region"), lax.axis_index("local")
    partner = {"region": region, "local": local ^ (n_local // 2)}
    exists = [local > 0, local < n_local - 1, region > 0, region < n_region - 1]
    peers = [
        {"region": region, "local": local - 1},
        {"region": region, "local": local + 1},
        {"region": region - 1, "local": local},
        {"region": region + 1, "local": local},
    ]

    barrier = pltpu.get_barrier_semaphore()
    pl.semaphore_signal(barrier, inc=1, device_id=partner, device_id_type=MESH)
    for t in range(4):

        @pl.when(exists[t])
        def _():
            pl.semaphore_signal(barrier, inc=1, device_id=peers[t], device_id_type=MESH)

    pl.semaphore_wait(barrier, 1 + sum(e.astype(jnp.int32) for e in exists))

    edge_copy = pltpu.make_async_remote_copy(
        src_ref=edge_ref,
        dst_ref=arr_edge,
        send_sem=edge_sems.at[0],
        recv_sem=edge_sems.at[1],
        device_id=partner,
        device_id_type=MESH,
    )
    inner_copies = [
        pltpu.make_async_remote_copy(
            src_ref=inner_ref.at[pl.ds(lo, hi - lo)],
            dst_ref=arr_inner.at[pl.ds(lo, hi - lo)],
            send_sem=inner_send.at[k],
            recv_sem=inner_recv.at[k],
            device_id=partner,
            device_id_type=MESH,
        )
        for k, (lo, hi) in enumerate(GROUPS)
    ]
    edge_copy.start()
    inner_copies[0].start()

    moved = move_ref[0, 0]
    slots = [
        jnp.where(moved == 0, 1, 0),
        jnp.where(moved == 2, 1, 2),
        moved,
    ]

    def place_of(link):
        slot = link // 2
        place = jnp.where(slot == moved, 2, slot - (slot > moved).astype(jnp.int32))
        return jnp.where(link < 6, 2 * place + link % 2, link)

    links = [place_of(link_ref[0, 2 * slots[c] + s]) for c in range(3) for s in range(2)]

    row16 = lax.broadcasted_iota(jnp.int32, (EDGE, PLANE), 0)
    row8 = lax.broadcasted_iota(jnp.int32, (HALF, PLANE), 0)
    low = row8 < QUARTER

    for pool in pools:
        pool[0:6] = jnp.zeros((6, 8, PLANE), jnp.float32)
        for j in range(2):
            pool[10 + j, 0:5, :] = bound_ref[j]
        for t in range(4):

            @pl.when(jnp.logical_not(exists[t]))
            def _():
                pool[6 + t] = jnp.zeros((8, PLANE), jnp.float32)

    def make_code(slot, c):
        lane = lax.broadcasted_iota(jnp.int32, (EDGE, PLANE), 1)
        y, z = lane // EDGE, lane % EDGE
        flags = jnp.where(fluid_ref[slot] > 0, 1, 0)
        up = jnp.where(row16 == 0, flags, pltpu.roll(flags, 1, 0))
        down = jnp.where(row16 == EDGE - 1, flags, pltpu.roll(flags, EDGE - 1, 0))
        code = jnp.left_shift(flags, POPS)
        for i, (cx, cy, cz) in enumerate(VELOCITIES):
            source = up if cx == 1 else down if cx == -1 else flags
            offset = (cy * EDGE + cz) % PLANE
            if offset:
                source = pltpu.roll(source, offset, 1)
            for axis, step in ((y, cy), (z, cz)):
                if step == 1:
                    source = jnp.where(axis == 0, 0, source)
                if step == -1:
                    source = jnp.where(axis == EDGE - 1, 0, source)
            code = code | jnp.left_shift(source & flags, i)
        code_ref[c] = code

    def collide_tiles(load, c):
        def tile(t, carry):
            rows = pl.ds(pl.multiple_of(t * HALF, HALF), HALF)
            post = collide([load(i, rows) for i in range(POPS)])
            for i in range(POPS):
                post_ref[c, i, rows, :] = post[i]
            return carry

        lax.fori_loop(0, 2, tile, 0)

    def stream(load, store, code, rows, pool, lower, upper):
        row = row16 if rows == EDGE else row8
        fluid = (code & (1 << POPS)) != 0
        for i, (cx, cy, cz) in enumerate(VELOCITIES):
            value = load(i)
            if cx == 1:
                j = PLUS_POPS.index(i)
                value = jnp.where(row == 0, pool[lower, j : j + 1, :], pltpu.roll(value, 1, 0))
            elif cx == -1:
                j = MINUS_POPS.index(i)
                edge = pool[upper, j : j + 1, :]
                value = jnp.where(row == rows - 1, edge, pltpu.roll(value, rows - 1, 0))
            offset = (cy * EDGE + cz) % PLANE
            if offset:
                value = pltpu.roll(value, offset, 1)
            if i == 0:
                store(i, jnp.where(fluid, value, 0.0))
            else:
                bounced = jnp.where(fluid, load(OPPOSITE[i]), 0.0)
                store(i, jnp.where((code & (1 << i)) != 0, value, bounced))

    def planes(pool, c, load):
        for s, pops in enumerate((MINUS_POPS, PLUS_POPS)):
            for j, i in enumerate(pops):
                pool[2 * c + s, j : j + 1, :] = load(i, s)

    def port_copy(it, t, peer):
        return pltpu.make_async_remote_copy(
            src_ref=ports.at[it, t],
            dst_ref=pools[it].at[6 + (t ^ 1)],
            send_sem=port_send.at[it, t],
            recv_sem=port_recv.at[it, t ^ 1],
            device_id=peer,
            device_id_type=MESH,
        )

    def send_ports(it):
        own = [pools[it][f] for f in range(6)]
        for t in range(4):
            plane = jnp.zeros((8, PLANE), jnp.float32)
            for f in range(6):
                plane = jnp.where(links[f] == 6 + t, own[f], plane)
            ports[it, t] = plane
        for t in range(4):

            @pl.when(exists[t])
            def _():
                port_copy(it, t, peers[t]).start()

    def wait_ports(it):
        for t in range(4):

            @pl.when(exists[t])
            def _():
                port_copy(it, t, peers[t]).wait_send()
                port_copy(it, t ^ 1, peers[t]).wait_recv()

    def kept_slot(c):
        return jnp.where(c == 0, slots[0], slots[1])

    def for_kept(body):
        def step(c, carry):
            body(c)
            return carry

        lax.fori_loop(0, 2, step, 0)

    def stream_kept(it, target):
        def body(c):
            lower = jnp.where(c == 0, links[0], links[2])
            upper = jnp.where(c == 0, links[1], links[3])

            def store(i, value):
                target[c, i] = value

            stream(lambda i: post_ref[c, i], store, code_ref[c], EDGE, pools[it], lower, upper)

        for_kept(body)

    def kept_planes(it):
        for c in range(2):
            planes(
                pools[it],
                c,
                lambda i, s: post_ref[c, i, (EDGE - 1) * s : (EDGE - 1) * s + 1, :],
            )

    def slab_step(it, source):
        post = collide([source[i] for i in range(POPS)])
        for i in range(POPS):
            slab_post_ref[i] = post[i]
        planes(
            pools[it],
            2,
            lambda i, s: slab_post_ref[i, (HALF - 1) * s : (HALF - 1) * s + 1, :],
        )

    def first(c):
        slot = kept_slot(c)
        collide_tiles(lambda i, rows: dist_ref[slot, i, rows, :], c)
        make_code(slot, c)

    for_kept(first)
    make_code(moved, 2)
    kept_planes(0)

    edge_copy.wait_recv()
    slab_step(0, arr_edge)
    send_ports(0)
    inner_copies[1].start()
    wait_ports(0)

    slab_code = jnp.where(low, code_ref[2, 0:HALF, :], code_ref[2, HALF:EDGE, :])

    def store_slab(i, value):
        slab_ref[i] = value

    stream(lambda i: slab_post_ref[i], store_slab, slab_code, HALF, pools[0], links[4], links[5])
    stream_kept(0, g_ref)
    slab_step(1, slab_ref)
    for_kept(lambda c: collide_tiles(lambda i, rows: g_ref[c, i, rows, :], c))
    kept_planes(1)
    send_ports(1)
    inner_copies[2].start()
    wait_ports(1)
    stream_kept(1, out_ref)

    for copy in inner_copies:
        copy.wait_recv()
    for i in range(POPS):
        turned = pltpu.roll(arr_inner[i], QUARTER, 0)
        g_ref[2, i, 0:HALF, :] = jnp.where(low, arr_edge[i], turned)
        g_ref[2, i, HALF:EDGE, :] = jnp.where(low, turned, arr_edge[i])

    def store_moved(i, value):
        g_ref[2, i] = value

    def store_out(i, value):
        out_ref[2, i] = value

    for it, store in ((0, store_moved), (1, store_out)):
        collide_tiles(lambda i, rows: g_ref[2, i, rows, :], 2)
        stream(lambda i: post_ref[2, i], store, code_ref[2], EDGE, pools[it], links[4], links[5])

    edge_copy.wait_send()
    for copy in inner_copies:
        copy.wait_send()


def on_device(n_region, n_local, distributions, fluid, boundary, face_link, move_slot):
    blocks, pops, sites = distributions.shape
    moved = move_slot[0, 0]
    outgoing = lax.dynamic_index_in_dim(distributions, moved, 0, keepdims=False)
    cut = sites // 4
    edge = jnp.concatenate([outgoing[:, :cut], outgoing[:, 3 * cut :]], 1)
    inner = outgoing[:, cut : 3 * cut]
    edge = edge.reshape(pops, HALF, PLANE)
    inner = inner.reshape(pops, HALF, PLANE)
    vmem = pl.BlockSpec(memory_space=pltpu.VMEM)
    smem = pl.BlockSpec(memory_space=pltpu.SMEM)
    f32 = jnp.float32
    result = pl.pallas_call(
        functools.partial(kernel, n_region, n_local),
        out_shape=jax.ShapeDtypeStruct((blocks, pops, EDGE, PLANE), f32),
        in_specs=[smem, smem, vmem, vmem, vmem, vmem, vmem],
        out_specs=vmem,
        scratch_shapes=[
            pltpu.VMEM((blocks, pops, EDGE, PLANE), f32),
            pltpu.VMEM((blocks, pops, EDGE, PLANE), f32),
            pltpu.VMEM((pops, HALF, PLANE), f32),
            pltpu.VMEM((pops, HALF, PLANE), f32),
            pltpu.VMEM((blocks, EDGE, PLANE), jnp.int32),
            pltpu.VMEM((pops, HALF, PLANE), f32),
            pltpu.VMEM((pops, HALF, PLANE), f32),
            pltpu.VMEM((12, 8, PLANE), f32),
            pltpu.VMEM((12, 8, PLANE), f32),
            pltpu.VMEM((ITERS, 4, 8, PLANE), f32),
            pltpu.SemaphoreType.DMA((2,)),
            pltpu.SemaphoreType.DMA((len(GROUPS),)),
            pltpu.SemaphoreType.DMA((len(GROUPS),)),
            pltpu.SemaphoreType.DMA((ITERS, 4)),
            pltpu.SemaphoreType.DMA((ITERS, 4)),
        ],
        compiler_params=pltpu.CompilerParams(collective_id=0, has_side_effects=True),
        name="two_steps",
    )(
        face_link,
        move_slot,
        distributions.reshape(blocks, pops, EDGE, PLANE),
        edge,
        inner,
        fluid.reshape(blocks, EDGE, PLANE),
        boundary[0],
    )
    first, second, last = result[0], result[1], result[2]
    ordered = jnp.stack(
        [
            jnp.where(moved == 0, last, first),
            jnp.where(moved == 1, last, jnp.where(moved == 0, first, second)),
            jnp.where(moved == 2, last, second),
        ]
    )
    return ordered.reshape(blocks, pops, sites)


def solution(mesh):
    in_specs = (
        P(("region", "local"), None, None),
        P(("region", "local"), None),
        P(("region", "local"), None, None, None),
        P(("region", "local"), None),
        P(("region", "local"), None),
    )
    out_specs = P(("region", "local"), None, None)
    body = functools.partial(on_device, mesh.shape["region"], mesh.shape["local"])
    return jax.shard_map(
        body, mesh=mesh, in_specs=in_specs, out_specs=out_specs, check_vma=False
    )
```

```python
import functools

import jax
import jax.numpy as jnp
from jax import lax
from jax.experimental import pallas as pl
from jax.experimental.pallas import tpu as pltpu
from jax.sharding import PartitionSpec as P

EDGE = 16
ITERS = 2
PLANE = EDGE * EDGE
HALF = EDGE // 2
QUARTER = EDGE // 4
MESH = pl.DeviceIdType.MESH

VELOCITIES = [
    (0, 0, 0),
    (1, 0, 0),
    (-1, 0, 0),
    (0, 1, 0),
    (0, -1, 0),
    (0, 0, 1),
    (0, 0, -1),
    (1, 1, 0),
    (-1, -1, 0),
    (1, -1, 0),
    (-1, 1, 0),
    (1, 0, 1),
    (-1, 0, -1),
    (1, 0, -1),
    (-1, 0, 1),
    (0, 1, 1),
    (0, -1, -1),
    (0, 1, -1),
    (0, -1, 1),
]
OPPOSITE = [0, 2, 1, 4, 3, 6, 5, 8, 7, 10, 9, 12, 11, 14, 13, 16, 15, 18, 17]
PLUS_POPS = [1, 7, 9, 11, 13]
MINUS_POPS = [2, 10, 8, 14, 12]
POPS = 19
BANDS = [(0, 8), (8, 16), (16, 19)]
GROUPS = [(0, 7), (7, 13), (13, 19)]


def collide(g):
    near = (g[1] + g[2]) + (g[3] + g[4]) + (g[5] + g[6])
    pair = {i: g[i] + g[i + 1] for i in range(7, POPS, 2)}
    diff = {i: g[i] - g[i + 1] for i in range(1, POPS, 2)}
    far = (pair[7] + pair[9]) + (pair[11] + pair[13]) + (pair[15] + pair[17])
    rho = (1.0 / 3.0) * g[0] + (1.0 / 18.0) * near + (1.0 / 36.0) * far
    ux = (1.0 / 18.0) * diff[1] + (1.0 / 36.0) * ((diff[7] + diff[9]) + (diff[11] + diff[13]))
    uy = (1.0 / 18.0) * diff[3] + (1.0 / 36.0) * ((diff[7] - diff[9]) + (diff[15] + diff[17]))
    uz = (1.0 / 18.0) * diff[5] + (1.0 / 36.0) * ((diff[11] - diff[13]) + (diff[15] - diff[17]))
    base = 1.6 * rho - 2.4 * (ux * ux + uy * uy + uz * uz)
    post = [base - 0.6 * g[0]]
    flows = [ux, uy, uz, ux + uy, ux - uy, ux + uz, ux - uz, uy + uz, uy - uz]
    for k, flow in enumerate(flows):
        i = 1 + 2 * k
        even = base + 7.2 * (flow * flow)
        odd = 4.8 * flow
        post.append((even + odd) - 0.6 * g[i])
        post.append((even - odd) - 0.6 * g[i + 1])
    return post


def kernel(
    n_region,
    n_local,
    link_hbm,
    move_ref,
    dist_ref,
    fluid_hbm,
    bound_hbm,
    kept_hbm,
    moved_ref,
    kept_ref,
    link_ref,
    fluid_ref,
    bound_ref,
    raw_ref,
    edge_ref,
    inner_ref,
    post_ref,
    g_ref,
    slab_ref,
    slab_post_ref,
    code_ref,
    arr_edge,
    arr_inner,
    pool0,
    pool1,
    ports,
    load_sems,
    small_sems,
    edge_sems,
    inner_send,
    inner_recv,
    port_send,
    port_recv,
):
    pools = [pool0, pool1]
    region, local = lax.axis_index("region"), lax.axis_index("local")
    partner = {"region": region, "local": local ^ (n_local // 2)}
    exists = [local > 0, local < n_local - 1, region > 0, region < n_region - 1]
    peers = [
        {"region": region, "local": local - 1},
        {"region": region, "local": local + 1},
        {"region": region - 1, "local": local},
        {"region": region + 1, "local": local},
    ]

    loads = [
        pltpu.make_async_copy(dist_ref.at[b], raw_ref.at[b], load_sems.at[b])
        for b in range(dist_ref.shape[0])
    ]
    small = [
        pltpu.make_async_copy(link_hbm, link_ref, small_sems.at[0]),
        pltpu.make_async_copy(fluid_hbm, fluid_ref, small_sems.at[1]),
        pltpu.make_async_copy(bound_hbm, bound_ref, small_sems.at[2]),
    ]
    for load in loads + small:
        load.start()

    barrier = pltpu.get_barrier_semaphore()
    pl.semaphore_signal(barrier, inc=1, device_id=partner, device_id_type=MESH)
    for t in range(4):

        @pl.when(exists[t])
        def _():
            pl.semaphore_signal(barrier, inc=1, device_id=peers[t], device_id_type=MESH)

    moved = move_ref[0, 0]
    slots = [
        jnp.where(moved == 0, 1, 0),
        jnp.where(moved == 2, 1, 2),
        moved,
    ]
    row16 = lax.broadcasted_iota(jnp.int32, (EDGE, PLANE), 0)
    row8 = lax.broadcasted_iota(jnp.int32, (HALF, PLANE), 0)
    low = row8 < QUARTER

    for load in loads:
        load.wait()
    for lo, hi in BANDS:
        part = raw_ref[moved, lo:hi, :].reshape(hi - lo, EDGE, PLANE)
        for i in range(lo, hi):
            edge_ref[i] = jnp.where(low, part[i - lo, :HALF], part[i - lo, HALF:])
            inner_ref[i] = jnp.where(low, part[i - lo, HALF:], part[i - lo, :HALF])

    pl.semaphore_wait(barrier, 1 + sum(e.astype(jnp.int32) for e in exists))

    edge_copy = pltpu.make_async_remote_copy(
        src_ref=edge_ref,
        dst_ref=arr_edge,
        send_sem=edge_sems.at[0],
        recv_sem=edge_sems.at[1],
        device_id=partner,
        device_id_type=MESH,
    )
    inner_copies = [
        pltpu.make_async_remote_copy(
            src_ref=inner_ref.at[pl.ds(lo, hi - lo)],
            dst_ref=arr_inner.at[pl.ds(lo, hi - lo)],
            send_sem=inner_send.at[k],
            recv_sem=inner_recv.at[k],
            device_id=partner,
            device_id_type=MESH,
        )
        for k, (lo, hi) in enumerate(GROUPS)
    ]
    edge_copy.start()
    inner_copies[0].start()

    for load in small:
        load.wait()

    def place_of(link):
        slot = link // 2
        place = jnp.where(slot == moved, 2, slot - (slot > moved).astype(jnp.int32))
        return jnp.where(link < 6, 2 * place + link % 2, link)

    links = [place_of(link_ref[0, 2 * slots[c] + s]) for c in range(3) for s in range(2)]

    for pool in pools:
        pool[0:6] = jnp.zeros((6, 8, PLANE), jnp.float32)
        for j in range(2):
            for k in range(5):
                pool[10 + j, k : k + 1, :] = bound_ref[0, k, j : j + 1, :]
        for t in range(4):

            @pl.when(jnp.logical_not(exists[t]))
            def _():
                pool[6 + t] = jnp.zeros((8, PLANE), jnp.float32)

    def make_code(slot, c):
        lane = lax.broadcasted_iota(jnp.int32, (EDGE, PLANE), 1)
        y, z = lane // EDGE, lane % EDGE
        flags = jnp.where(fluid_ref[pl.ds(slot, 1), :].reshape(EDGE, PLANE) > 0, 1, 0)
        up = jnp.where(row16 == 0, flags, pltpu.roll(flags, 1, 0))
        down = jnp.where(row16 == EDGE - 1, flags, pltpu.roll(flags, EDGE - 1, 0))
        code = jnp.left_shift(flags, POPS)
        for i, (cx, cy, cz) in enumerate(VELOCITIES):
            source = up if cx == 1 else down if cx == -1 else flags
            offset = (cy * EDGE + cz) % PLANE
            if offset:
                source = pltpu.roll(source, offset, 1)
            for axis, step in ((y, cy), (z, cz)):
                if step == 1:
                    source = jnp.where(axis == 0, 0, source)
                if step == -1:
                    source = jnp.where(axis == EDGE - 1, 0, source)
            code = code | jnp.left_shift(source & flags, i)
        code_ref[c] = code

    def collide_tiles(load, c):
        def tile(t, carry):
            rows = pl.ds(pl.multiple_of(t * HALF, HALF), HALF)
            post = collide([load(i, rows) for i in range(POPS)])
            for i in range(POPS):
                post_ref[c, i, rows, :] = post[i]
            return carry

        lax.fori_loop(0, 2, tile, 0)

    def stream(load, store, code, rows, pool, lower, upper):
        row = row16 if rows == EDGE else row8
        fluid = (code & (1 << POPS)) != 0
        for i, (cx, cy, cz) in enumerate(VELOCITIES):
            value = load(i)
            if cx == 1:
                j = PLUS_POPS.index(i)
                value = jnp.where(row == 0, pool[lower, j : j + 1, :], pltpu.roll(value, 1, 0))
            elif cx == -1:
                j = MINUS_POPS.index(i)
                edge = pool[upper, j : j + 1, :]
                value = jnp.where(row == rows - 1, edge, pltpu.roll(value, rows - 1, 0))
            offset = (cy * EDGE + cz) % PLANE
            if offset:
                value = pltpu.roll(value, offset, 1)
            if i == 0:
                store(i, jnp.where(fluid, value, 0.0))
            else:
                bounced = jnp.where(fluid, load(OPPOSITE[i]), 0.0)
                store(i, jnp.where((code & (1 << i)) != 0, value, bounced))

    def planes(pool, c, load):
        for s, pops in enumerate((MINUS_POPS, PLUS_POPS)):
            for j, i in enumerate(pops):
                pool[2 * c + s, j : j + 1, :] = load(i, s)

    def port_copy(it, t, peer):
        return pltpu.make_async_remote_copy(
            src_ref=ports.at[it, t],
            dst_ref=pools[it].at[6 + (t ^ 1)],
            send_sem=port_send.at[it, t],
            recv_sem=port_recv.at[it, t ^ 1],
            device_id=peer,
            device_id_type=MESH,
        )

    def send_ports(it):
        own = [pools[it][f] for f in range(6)]
        for t in range(4):
            plane = jnp.zeros((8, PLANE), jnp.float32)
            for f in range(6):
                plane = jnp.where(links[f] == 6 + t, own[f], plane)
            ports[it, t] = plane
        for t in range(4):

            @pl.when(exists[t])
            def _():
                port_copy(it, t, peers[t]).start()

    def wait_ports(it):
        for t in range(4):

            @pl.when(exists[t])
            def _():
                port_copy(it, t, peers[t]).wait_send()
                port_copy(it, t ^ 1, peers[t]).wait_recv()

    def kept_slot(c):
        return jnp.where(c == 0, slots[0], slots[1])

    def for_kept(body):
        def step(c, carry):
            body(c)
            return carry

        lax.fori_loop(0, 2, step, 0)

    def stream_kept(it, target):
        def body(c):
            lower = jnp.where(c == 0, links[0], links[2])
            upper = jnp.where(c == 0, links[1], links[3])

            def store(i, value):
                target[c, i] = value

            stream(lambda i: post_ref[c, i], store, code_ref[c], EDGE, pools[it], lower, upper)

        for_kept(body)

    def kept_planes(it):
        for c in range(2):
            planes(
                pools[it],
                c,
                lambda i, s: post_ref[c, i, (EDGE - 1) * s : (EDGE - 1) * s + 1, :],
            )

    def slab_step(it, source):
        post = collide([source[i] for i in range(POPS)])
        for i in range(POPS):
            slab_post_ref[i] = post[i]
        planes(
            pools[it],
            2,
            lambda i, s: slab_post_ref[i, (HALF - 1) * s : (HALF - 1) * s + 1, :],
        )

    def first(c):
        slot = kept_slot(c)
        for lo, hi in BANDS:
            g_ref[c, lo:hi] = raw_ref[slot, lo:hi, :].reshape(hi - lo, EDGE, PLANE)
        collide_tiles(lambda i, rows: g_ref[c, i, rows, :], c)
        make_code(slot, c)

    for_kept(first)
    make_code(moved, 2)
    kept_planes(0)

    edge_copy.wait_recv()
    slab_step(0, arr_edge)
    send_ports(0)
    inner_copies[1].start()
    wait_ports(0)

    slab_code = jnp.where(low, code_ref[2, 0:HALF, :], code_ref[2, HALF:EDGE, :])

    def store_slab(i, value):
        slab_ref[i] = value

    stream(lambda i: slab_post_ref[i], store_slab, slab_code, HALF, pools[0], links[4], links[5])
    stream_kept(0, g_ref)
    slab_step(1, slab_ref)
    for_kept(lambda c: collide_tiles(lambda i, rows: g_ref[c, i, rows, :], c))
    kept_planes(1)
    send_ports(1)
    inner_copies[2].start()
    wait_ports(1)
    stream_kept(1, g_ref)
    for c in range(2):
        for lo, hi in BANDS:
            kept_ref[c, lo:hi, :] = g_ref[c, lo:hi].reshape(hi - lo, EDGE * PLANE)

    kept_out = pltpu.make_async_copy(kept_ref, kept_hbm, small_sems.at[3])
    kept_out.start()

    for copy in inner_copies:
        copy.wait_recv()
    for i in range(POPS):
        g_ref[2, i, 0:HALF, :] = jnp.where(low, arr_edge[i], arr_inner[i])
        g_ref[2, i, HALF:EDGE, :] = jnp.where(low, arr_inner[i], arr_edge[i])

    def store_moved(i, value):
        g_ref[2, i] = value

    def store_out(i, value):
        moved_ref[i] = value

    for it, store in ((0, store_moved), (1, store_out)):
        collide_tiles(lambda i, rows: g_ref[2, i, rows, :], 2)
        stream(lambda i: post_ref[2, i], store, code_ref[2], EDGE, pools[it], links[4], links[5])

    kept_out.wait()
    edge_copy.wait_send()
    for copy in inner_copies:
        copy.wait_send()


def place_kernel(move_ref, kept_hbm, moved_hbm, out_ref, kept_ref, moved_ref, flat_ref, sems):
    moved = move_ref[0, 0]
    loads = [
        pltpu.make_async_copy(moved_hbm, moved_ref, sems.at[0]),
        pltpu.make_async_copy(kept_hbm.at[0], kept_ref.at[0], sems.at[1]),
        pltpu.make_async_copy(kept_hbm.at[1], kept_ref.at[1], sems.at[2]),
    ]
    stores = [
        pltpu.make_async_copy(flat_ref, out_ref.at[moved], sems.at[3]),
        pltpu.make_async_copy(kept_ref.at[0], out_ref.at[jnp.where(moved == 0, 1, 0)], sems.at[4]),
        pltpu.make_async_copy(kept_ref.at[1], out_ref.at[jnp.where(moved == 2, 1, 2)], sems.at[5]),
    ]
    for load in loads:
        load.start()
    loads[0].wait()
    for lo, hi in BANDS:
        flat_ref[lo:hi, :] = moved_ref[lo:hi].reshape(hi - lo, EDGE * PLANE)
    stores[0].start()
    for load, store in zip(loads[1:], stores[1:]):
        load.wait()
        store.start()
    for store in stores:
        store.wait()


def on_device(n_region, n_local, distributions, fluid, boundary, face_link, move_slot):
    blocks, pops, sites = distributions.shape
    vmem = pl.BlockSpec(memory_space=pltpu.VMEM)
    smem = pl.BlockSpec(memory_space=pltpu.SMEM)
    hbm = pl.BlockSpec(memory_space=pltpu.HBM)
    f32 = jnp.float32
    bound = boundary.transpose(0, 2, 1, 3)
    kept, moved = pl.pallas_call(
        functools.partial(kernel, n_region, n_local),
        out_shape=[
            jax.ShapeDtypeStruct((blocks - 1, pops, sites), f32),
            jax.ShapeDtypeStruct((pops, EDGE, PLANE), f32),
        ],
        in_specs=[hbm, smem, hbm, hbm, hbm],
        out_specs=[hbm, vmem],
        scratch_shapes=[
            pltpu.VMEM((blocks - 1, pops, sites), f32),
            pltpu.SMEM(face_link.shape, jnp.int32),
            pltpu.VMEM(fluid.shape, jnp.int32),
            pltpu.VMEM(bound.shape, f32),
            pltpu.VMEM((blocks, pops, sites), f32),
            pltpu.VMEM((pops, HALF, PLANE), f32),
            pltpu.VMEM((pops, HALF, PLANE), f32),
            pltpu.VMEM((blocks, pops, EDGE, PLANE), f32),
            pltpu.VMEM((blocks, pops, EDGE, PLANE), f32),
            pltpu.VMEM((pops, HALF, PLANE), f32),
            pltpu.VMEM((pops, HALF, PLANE), f32),
            pltpu.VMEM((blocks, EDGE, PLANE), jnp.int32),
            pltpu.VMEM((pops, HALF, PLANE), f32),
            pltpu.VMEM((pops, HALF, PLANE), f32),
            pltpu.VMEM((12, 8, PLANE), f32),
            pltpu.VMEM((12, 8, PLANE), f32),
            pltpu.VMEM((ITERS, 4, 8, PLANE), f32),
            pltpu.SemaphoreType.DMA((blocks,)),
            pltpu.SemaphoreType.DMA((4,)),
            pltpu.SemaphoreType.DMA((2,)),
            pltpu.SemaphoreType.DMA((len(GROUPS),)),
            pltpu.SemaphoreType.DMA((len(GROUPS),)),
            pltpu.SemaphoreType.DMA((ITERS, 4)),
            pltpu.SemaphoreType.DMA((ITERS, 4)),
        ],
        compiler_params=pltpu.CompilerParams(collective_id=0, has_side_effects=True),
        name="two_steps",
    )(face_link, move_slot, distributions, fluid, bound)
    return pl.pallas_call(
        place_kernel,
        out_shape=jax.ShapeDtypeStruct((blocks, pops, sites), f32),
        in_specs=[smem, hbm, hbm],
        out_specs=hbm,
        scratch_shapes=[
            pltpu.VMEM(kept.shape, f32),
            pltpu.VMEM(moved.shape, f32),
            pltpu.VMEM((pops, sites), f32),
            pltpu.SemaphoreType.DMA((6,)),
        ],
        name="place",
    )(move_slot, kept, moved)


def solution(mesh):
    in_specs = (
        P(("region", "local"), None, None),
        P(("region", "local"), None),
        P(("region", "local"), None, None, None),
        P(("region", "local"), None),
        P(("region", "local"), None),
    )
    out_specs = P(("region", "local"), None, None)
    body = functools.partial(on_device, mesh.shape["region"], mesh.shape["local"])
    return jax.shard_map(
        body, mesh=mesh, in_specs=in_specs, out_specs=out_specs, check_vma=False
    )
```

```python
import functools

import jax
import jax.numpy as jnp
from jax import lax
from jax.experimental import pallas as pl
from jax.experimental.pallas import tpu as pltpu
from jax.sharding import PartitionSpec as P

EDGE = 16
ITERS = 2
PLANE = EDGE * EDGE
HALF = EDGE // 2
QUARTER = EDGE // 4
MESH = pl.DeviceIdType.MESH

VELOCITIES = [
    (0, 0, 0),
    (1, 0, 0),
    (-1, 0, 0),
    (0, 1, 0),
    (0, -1, 0),
    (0, 0, 1),
    (0, 0, -1),
    (1, 1, 0),
    (-1, -1, 0),
    (1, -1, 0),
    (-1, 1, 0),
    (1, 0, 1),
    (-1, 0, -1),
    (1, 0, -1),
    (-1, 0, 1),
    (0, 1, 1),
    (0, -1, -1),
    (0, 1, -1),
    (0, -1, 1),
]
OPPOSITE = [0, 2, 1, 4, 3, 6, 5, 8, 7, 10, 9, 12, 11, 14, 13, 16, 15, 18, 17]
PLUS_POPS = [1, 7, 9, 11, 13]
MINUS_POPS = [2, 10, 8, 14, 12]
POPS = 19
BANDS = [(0, 8), (8, 16), (16, 19)]
GROUPS = [(0, 7), (7, 14), (14, 19)]


def collide(g):
    near = (g[1] + g[2]) + (g[3] + g[4]) + (g[5] + g[6])
    pair = {i: g[i] + g[i + 1] for i in range(7, POPS, 2)}
    diff = {i: g[i] - g[i + 1] for i in range(1, POPS, 2)}
    far = (pair[7] + pair[9]) + (pair[11] + pair[13]) + (pair[15] + pair[17])
    rho = (1.0 / 3.0) * g[0] + (1.0 / 18.0) * near + (1.0 / 36.0) * far
    ux = (1.0 / 18.0) * diff[1] + (1.0 / 36.0) * ((diff[7] + diff[9]) + (diff[11] + diff[13]))
    uy = (1.0 / 18.0) * diff[3] + (1.0 / 36.0) * ((diff[7] - diff[9]) + (diff[15] + diff[17]))
    uz = (1.0 / 18.0) * diff[5] + (1.0 / 36.0) * ((diff[11] - diff[13]) + (diff[15] - diff[17]))
    base = 1.6 * rho - 2.4 * (ux * ux + uy * uy + uz * uz)
    post = [base - 0.6 * g[0]]
    flows = [ux, uy, uz, ux + uy, ux - uy, ux + uz, ux - uz, uy + uz, uy - uz]
    for k, flow in enumerate(flows):
        i = 1 + 2 * k
        even = base + 7.2 * (flow * flow)
        odd = 4.8 * flow
        post.append((even + odd) - 0.6 * g[i])
        post.append((even - odd) - 0.6 * g[i + 1])
    return post


def kernel(
    n_region,
    n_local,
    link_hbm,
    move_ref,
    dist_ref,
    fluid_hbm,
    bound_hbm,
    kept_hbm,
    moved_ref,
    kept_ref,
    link_ref,
    fluid_ref,
    bound_ref,
    raw_ref,
    edge_ref,
    inner_ref,
    post_ref,
    g_ref,
    slab_ref,
    slab_post_ref,
    code_ref,
    arr_edge,
    arr_inner,
    pool0,
    pool1,
    ports,
    load_sems,
    small_sems,
    edge_sems,
    inner_send,
    inner_recv,
    port_send,
    port_recv,
):
    pools = [pool0, pool1]
    region, local = lax.axis_index("region"), lax.axis_index("local")
    partner = {"region": region, "local": local ^ (n_local // 2)}
    exists = [local > 0, local < n_local - 1, region > 0, region < n_region - 1]
    peers = [
        {"region": region, "local": local - 1},
        {"region": region, "local": local + 1},
        {"region": region - 1, "local": local},
        {"region": region + 1, "local": local},
    ]

    loads = [
        pltpu.make_async_copy(dist_ref.at[b], raw_ref.at[b], load_sems.at[b])
        for b in range(dist_ref.shape[0])
    ]
    small = [
        pltpu.make_async_copy(link_hbm, link_ref, small_sems.at[0]),
        pltpu.make_async_copy(fluid_hbm, fluid_ref, small_sems.at[1]),
        pltpu.make_async_copy(bound_hbm, bound_ref, small_sems.at[2]),
    ]
    for load in loads + small:
        load.start()

    barrier = pltpu.get_barrier_semaphore()
    pl.semaphore_signal(barrier, inc=1, device_id=partner, device_id_type=MESH)
    for t in range(4):

        @pl.when(exists[t])
        def _():
            pl.semaphore_signal(barrier, inc=1, device_id=peers[t], device_id_type=MESH)

    moved = move_ref[0, 0]
    slots = [
        jnp.where(moved == 0, 1, 0),
        jnp.where(moved == 2, 1, 2),
        moved,
    ]
    row16 = lax.broadcasted_iota(jnp.int32, (EDGE, PLANE), 0)
    row8 = lax.broadcasted_iota(jnp.int32, (HALF, PLANE), 0)
    low = row8 < QUARTER

    for load in loads:
        load.wait()
    for lo, hi in BANDS:
        part = raw_ref[moved, lo:hi, :].reshape(hi - lo, EDGE, PLANE)
        for i in range(lo, hi):
            edge_ref[i] = jnp.where(low, part[i - lo, :HALF], part[i - lo, HALF:])
            inner_ref[i] = jnp.where(low, part[i - lo, HALF:], part[i - lo, :HALF])

    pl.semaphore_wait(barrier, 1 + sum(e.astype(jnp.int32) for e in exists))

    edge_copy = pltpu.make_async_remote_copy(
        src_ref=edge_ref,
        dst_ref=arr_edge,
        send_sem=edge_sems.at[0],
        recv_sem=edge_sems.at[1],
        device_id=partner,
        device_id_type=MESH,
    )
    inner_copies = [
        pltpu.make_async_remote_copy(
            src_ref=inner_ref.at[pl.ds(lo, hi - lo)],
            dst_ref=arr_inner.at[pl.ds(lo, hi - lo)],
            send_sem=inner_send.at[k],
            recv_sem=inner_recv.at[k],
            device_id=partner,
            device_id_type=MESH,
        )
        for k, (lo, hi) in enumerate(GROUPS)
    ]
    edge_copy.start()
    inner_copies[0].start()

    for load in small:
        load.wait()

    def place_of(link):
        slot = link // 2
        place = jnp.where(slot == moved, 2, slot - (slot > moved).astype(jnp.int32))
        return jnp.where(link < 6, 2 * place + link % 2, link)

    links = [place_of(link_ref[0, 2 * slots[c] + s]) for c in range(3) for s in range(2)]

    for pool in pools:
        pool[0:6] = jnp.zeros((6, 8, PLANE), jnp.float32)
        for j in range(2):
            for k in range(5):
                pool[10 + j, k : k + 1, :] = bound_ref[0, k, j : j + 1, :]
        for t in range(4):

            @pl.when(jnp.logical_not(exists[t]))
            def _():
                pool[6 + t] = jnp.zeros((8, PLANE), jnp.float32)

    def make_code(slot, c):
        lane = lax.broadcasted_iota(jnp.int32, (EDGE, PLANE), 1)
        y, z = lane // EDGE, lane % EDGE
        flags = jnp.where(fluid_ref[pl.ds(slot, 1), :].reshape(EDGE, PLANE) > 0, 1, 0)
        up = jnp.where(row16 == 0, flags, pltpu.roll(flags, 1, 0))
        down = jnp.where(row16 == EDGE - 1, flags, pltpu.roll(flags, EDGE - 1, 0))
        code = jnp.left_shift(flags, POPS)
        for i, (cx, cy, cz) in enumerate(VELOCITIES):
            source = up if cx == 1 else down if cx == -1 else flags
            offset = (cy * EDGE + cz) % PLANE
            if offset:
                source = pltpu.roll(source, offset, 1)
            for axis, step in ((y, cy), (z, cz)):
                if step == 1:
                    source = jnp.where(axis == 0, 0, source)
                if step == -1:
                    source = jnp.where(axis == EDGE - 1, 0, source)
            code = code | jnp.left_shift(source & flags, i)
        code_ref[c] = code

    def collide_tiles(load, c):
        def tile(t, carry):
            rows = pl.ds(pl.multiple_of(t * HALF, HALF), HALF)
            post = collide([load(i, rows) for i in range(POPS)])
            for i in range(POPS):
                post_ref[c, i, rows, :] = post[i]
            return carry

        lax.fori_loop(0, 2, tile, 0)

    def stream(load, store, code, rows, pool, lower, upper):
        row = row16 if rows == EDGE else row8
        fluid = (code & (1 << POPS)) != 0
        for i, (cx, cy, cz) in enumerate(VELOCITIES):
            value = load(i)
            if cx == 1:
                j = PLUS_POPS.index(i)
                value = jnp.where(row == 0, pool[lower, j : j + 1, :], pltpu.roll(value, 1, 0))
            elif cx == -1:
                j = MINUS_POPS.index(i)
                edge = pool[upper, j : j + 1, :]
                value = jnp.where(row == rows - 1, edge, pltpu.roll(value, rows - 1, 0))
            offset = (cy * EDGE + cz) % PLANE
            if offset:
                value = pltpu.roll(value, offset, 1)
            if i == 0:
                store(i, jnp.where(fluid, value, 0.0))
            else:
                bounced = jnp.where(fluid, load(OPPOSITE[i]), 0.0)
                store(i, jnp.where((code & (1 << i)) != 0, value, bounced))

    def planes(pool, c, load):
        for s, pops in enumerate((MINUS_POPS, PLUS_POPS)):
            for j, i in enumerate(pops):
                pool[2 * c + s, j : j + 1, :] = load(i, s)

    def port_copy(it, t, peer):
        return pltpu.make_async_remote_copy(
            src_ref=ports.at[it, t],
            dst_ref=pools[it].at[6 + (t ^ 1)],
            send_sem=port_send.at[it, t],
            recv_sem=port_recv.at[it, t ^ 1],
            device_id=peer,
            device_id_type=MESH,
        )

    def send_ports(it):
        own = [pools[it][f] for f in range(6)]
        for t in range(4):
            plane = jnp.zeros((8, PLANE), jnp.float32)
            for f in range(6):
                plane = jnp.where(links[f] == 6 + t, own[f], plane)
            ports[it, t] = plane
        for t in range(4):

            @pl.when(exists[t])
            def _():
                port_copy(it, t, peers[t]).start()

    def wait_ports(it):
        for t in range(4):

            @pl.when(exists[t])
            def _():
                port_copy(it, t, peers[t]).wait_send()
                port_copy(it, t ^ 1, peers[t]).wait_recv()

    def kept_slot(c):
        return jnp.where(c == 0, slots[0], slots[1])

    def for_kept(body):
        def step(c, carry):
            body(c)
            return carry

        lax.fori_loop(0, 2, step, 0)

    def stream_kept(it, target):
        def body(c):
            lower = jnp.where(c == 0, links[0], links[2])
            upper = jnp.where(c == 0, links[1], links[3])

            def store(i, value):
                target[c, i] = value

            stream(lambda i: post_ref[c, i], store, code_ref[c], EDGE, pools[it], lower, upper)

        for_kept(body)

    def kept_planes(it):
        for c in range(2):
            planes(
                pools[it],
                c,
                lambda i, s: post_ref[c, i, (EDGE - 1) * s : (EDGE - 1) * s + 1, :],
            )

    def slab_step(it, source):
        post = collide([source[i] for i in range(POPS)])
        for i in range(POPS):
            slab_post_ref[it, i] = post[i]
        planes(
            pools[it],
            2,
            lambda i, s: slab_post_ref[it, i, (HALF - 1) * s : (HALF - 1) * s + 1, :],
        )

    def first(c):
        slot = kept_slot(c)
        for lo, hi in BANDS:
            g_ref[c, lo:hi] = raw_ref[slot, lo:hi, :].reshape(hi - lo, EDGE, PLANE)
        collide_tiles(lambda i, rows: g_ref[c, i, rows, :], c)
        make_code(slot, c)

    for_kept(first)
    make_code(moved, 2)
    kept_planes(0)

    edge_copy.wait_recv()
    slab_step(0, arr_edge)
    send_ports(0)
    inner_copies[1].start()
    wait_ports(0)

    slab_code = jnp.where(low, code_ref[2, 0:HALF, :], code_ref[2, HALF:EDGE, :])

    def store_slab(i, value):
        slab_ref[i] = value

    stream(lambda i: slab_post_ref[0, i], store_slab, slab_code, HALF, pools[0], links[4], links[5])
    stream_kept(0, g_ref)
    slab_step(1, slab_ref)
    for_kept(lambda c: collide_tiles(lambda i, rows: g_ref[c, i, rows, :], c))
    kept_planes(1)
    send_ports(1)
    inner_copies[2].start()
    wait_ports(1)
    stream_kept(1, g_ref)
    for c in range(2):
        for lo, hi in BANDS:
            kept_ref[c, lo:hi, :] = g_ref[c, lo:hi].reshape(hi - lo, EDGE * PLANE)

    kept_out = pltpu.make_async_copy(kept_ref, kept_hbm, small_sems.at[3])
    kept_out.start()

    for copy in inner_copies:
        copy.wait_recv()
    inner_post = collide([arr_inner[i] for i in range(POPS)])
    for i in range(POPS):
        edge_post = slab_post_ref[0, i]
        post_ref[2, i, 0:HALF, :] = jnp.where(low, edge_post, inner_post[i])
        post_ref[2, i, HALF:EDGE, :] = jnp.where(low, inner_post[i], edge_post)

    def store_moved(i, value):
        g_ref[2, i] = value

    def store_out(i, value):
        moved_ref[i] = value

    for it, store in ((0, store_moved), (1, store_out)):
        if it:
            collide_tiles(lambda i, rows: g_ref[2, i, rows, :], 2)
        stream(lambda i: post_ref[2, i], store, code_ref[2], EDGE, pools[it], links[4], links[5])

    kept_out.wait()
    edge_copy.wait_send()
    for copy in inner_copies:
        copy.wait_send()


def place_kernel(move_ref, kept_hbm, moved_hbm, out_ref, kept_ref, moved_ref, flat_ref, sems):
    moved = move_ref[0, 0]
    loads = [
        pltpu.make_async_copy(moved_hbm, moved_ref, sems.at[0]),
        pltpu.make_async_copy(kept_hbm.at[0], kept_ref.at[0], sems.at[1]),
        pltpu.make_async_copy(kept_hbm.at[1], kept_ref.at[1], sems.at[2]),
    ]
    stores = [
        pltpu.make_async_copy(flat_ref, out_ref.at[moved], sems.at[3]),
        pltpu.make_async_copy(kept_ref.at[0], out_ref.at[jnp.where(moved == 0, 1, 0)], sems.at[4]),
        pltpu.make_async_copy(kept_ref.at[1], out_ref.at[jnp.where(moved == 2, 1, 2)], sems.at[5]),
    ]
    for load in loads:
        load.start()
    loads[0].wait()
    for lo, hi in BANDS:
        flat_ref[lo:hi, :] = moved_ref[lo:hi].reshape(hi - lo, EDGE * PLANE)
    stores[0].start()
    for load, store in zip(loads[1:], stores[1:]):
        load.wait()
        store.start()
    for store in stores:
        store.wait()


def on_device(n_region, n_local, distributions, fluid, boundary, face_link, move_slot):
    blocks, pops, sites = distributions.shape
    vmem = pl.BlockSpec(memory_space=pltpu.VMEM)
    smem = pl.BlockSpec(memory_space=pltpu.SMEM)
    hbm = pl.BlockSpec(memory_space=pltpu.HBM)
    f32 = jnp.float32
    bound = boundary.transpose(0, 2, 1, 3)
    kept, moved = pl.pallas_call(
        functools.partial(kernel, n_region, n_local),
        out_shape=[
            jax.ShapeDtypeStruct((blocks - 1, pops, sites), f32),
            jax.ShapeDtypeStruct((pops, EDGE, PLANE), f32),
        ],
        in_specs=[hbm, smem, hbm, hbm, hbm],
        out_specs=[hbm, vmem],
        scratch_shapes=[
            pltpu.VMEM((blocks - 1, pops, sites), f32),
            pltpu.SMEM(face_link.shape, jnp.int32),
            pltpu.VMEM(fluid.shape, jnp.int32),
            pltpu.VMEM(bound.shape, f32),
            pltpu.VMEM((blocks, pops, sites), f32),
            pltpu.VMEM((pops, HALF, PLANE), f32),
            pltpu.VMEM((pops, HALF, PLANE), f32),
            pltpu.VMEM((blocks, pops, EDGE, PLANE), f32),
            pltpu.VMEM((blocks, pops, EDGE, PLANE), f32),
            pltpu.VMEM((pops, HALF, PLANE), f32),
            pltpu.VMEM((ITERS, pops, HALF, PLANE), f32),
            pltpu.VMEM((blocks, EDGE, PLANE), jnp.int32),
            pltpu.VMEM((pops, HALF, PLANE), f32),
            pltpu.VMEM((pops, HALF, PLANE), f32),
            pltpu.VMEM((12, 8, PLANE), f32),
            pltpu.VMEM((12, 8, PLANE), f32),
            pltpu.VMEM((ITERS, 4, 8, PLANE), f32),
            pltpu.SemaphoreType.DMA((blocks,)),
            pltpu.SemaphoreType.DMA((4,)),
            pltpu.SemaphoreType.DMA((2,)),
            pltpu.SemaphoreType.DMA((len(GROUPS),)),
            pltpu.SemaphoreType.DMA((len(GROUPS),)),
            pltpu.SemaphoreType.DMA((ITERS, 4)),
            pltpu.SemaphoreType.DMA((ITERS, 4)),
        ],
        compiler_params=pltpu.CompilerParams(collective_id=0, has_side_effects=True),
        name="two_steps",
    )(face_link, move_slot, distributions, fluid, bound)
    return pl.pallas_call(
        place_kernel,
        out_shape=jax.ShapeDtypeStruct((blocks, pops, sites), f32),
        in_specs=[smem, hbm, hbm],
        out_specs=hbm,
        scratch_shapes=[
            pltpu.VMEM(kept.shape, f32),
            pltpu.VMEM(moved.shape, f32),
            pltpu.VMEM((pops, sites), f32),
            pltpu.SemaphoreType.DMA((6,)),
        ],
        name="place",
    )(move_slot, kept, moved)


def solution(mesh):
    in_specs = (
        P(("region", "local"), None, None),
        P(("region", "local"), None),
        P(("region", "local"), None, None, None),
        P(("region", "local"), None),
        P(("region", "local"), None),
    )
    out_specs = P(("region", "local"), None, None)
    body = functools.partial(on_device, mesh.shape["region"], mesh.shape["local"])
    return jax.shard_map(
        body, mesh=mesh, in_specs=in_specs, out_specs=out_specs, check_vma=False
    )
```
